32 devices in a mesh: row: 8 (over z, core), col: 4 (over y, x).
Axes of the slice: x: 2, y: 2, z: 4, core: 2. Of those that a mesh axis runs over, the one named last changes fastest.
Arguments:
- pivot_inverse: float32 [1024, 1024], P('row'), may hold values from -1 to 2, as said below
- panel: float32 [16, 1024, 1024], P('row', 'col'), may hold values from -1 to 1
- trailing: float32 [160, 1024, 1024], P('row', None, 'col'), may hold values from -6 to 6
- tile_list: int32 [160, 2], P('row'), may hold values from -1 to 15, as said below
Outputs:
- solved_panel: float32 [16, 1024, 1024], P('row', 'col')
- updated: float32 [160, 1024, 1024], P('row', None, 'col')
The draws below stay inside these ranges and needn't reach their ends.
Inputs may be any that keep to these rules, and one draw needn't show every extreme that they name: `pivot_inverse`: lower triangular, diagonal between 0.5 and 2. `tile_list`: slots t of group g are g * 20 to g * 20 + 19. Column 0 lies in 0 to 1; column 1 is a panel tile or -1 for an empty slot. The live slots of a group come first and name distinct pairs; each group in the first half of the groups holds exactly 6 live slots, each in the second half exactly 20. Empty slots hold 0 in column 0.
All inputs are finite; a program needn't handle non-finite values.
Results may differ from the reference program's by a relative error of at most 0.00007.
Values sent between devices are 32-bit elements; how exact they have to be, the bound alone decides.
A program may use at most 128 MiB of HBM per device.

```python
import math
import jax
import jax.numpy as jnp
from jax import lax

B = 1024
PAN_DEV = 2
TR_DEV = 20
LIGHT = 6
PANEL = 16
TRAIL = 160


def draw_pivot_inverse(key, part):
    first_key, second_key = jax.random.split(key)
    lower_part = jnp.tril(jax.random.normal(first_key, (B, B), jnp.float32), -1) * (0.6 / math.sqrt(B))
    diagonal = jnp.exp(jax.random.uniform(second_key, (B,), jnp.float32, math.log(0.5), math.log(2.0)))
    return (lower_part + jnp.diag(diagonal)).astype(jnp.float32)


def draw_tile_list(key, part):
    groups = TRAIL // TR_DEV
    options = PAN_DEV * PANEL
    group_keys = jax.random.split(jax.random.fold_in(key, 7), groups)
    shuffled = jax.vmap(lambda one_key: jax.random.permutation(one_key, options))(group_keys)[:, :TR_DEV]
    local_tile = shuffled // PANEL
    paired_tile = shuffled % PANEL
    slot_index = jnp.arange(TR_DEV)[None, :]
    group_index = jnp.arange(groups)[:, None]
    live_count = jnp.where(group_index >= groups // 2, TR_DEV, LIGHT)
    live_slot = slot_index < live_count
    local_tile = jnp.where(live_slot, local_tile, 0)
    paired_tile = jnp.where(live_slot, paired_tile, -1)
    return jnp.stack([local_tile, paired_tile], -1).reshape(TRAIL, 2).astype(jnp.int32)


def steps_of(rng, extent, pieces, least, high):
    level, own = 1.0, jax.random.fold_in(rng, 6)
    for axis_at, shards_of in pieces:
        steps = jnp.exp(jax.random.uniform(jax.random.fold_in(own, axis_at), (shards_of,), jnp.float32, least / len(pieces), high / len(pieces)))
        level = level * jnp.repeat(steps, extent[axis_at] // shards_of).reshape([-1 if axis == axis_at else 1 for axis in range(len(extent))])
    return level


def noise(own_key, shape, deviation, reach, cuts=(), kind=jnp.bfloat16):
    loudness = steps_of(own_key, shape, cuts, -0.22, 0.18) if cuts else 1.0
    values = jax.random.normal(own_key, shape, jnp.float32) * deviation * loudness
    return jnp.minimum(jnp.maximum(values, -reach), reach).astype(kind)


def setup_inputs(seed: int = 0) -> dict:
    seeds = jax.random.split(jax.random.key(seed), 5)
    pivot_inverse = draw_pivot_inverse(jax.random.fold_in(seeds[4], 71), 0)
    panel = noise(seeds[1], (PANEL, B, B), 0.18, 1.0, ((0, 8), (1, 4)), jnp.float32)
    trailing = noise(seeds[2], (TRAIL, B, B), 1.0, 6.0, ((0, 8), (2, 4)), jnp.float32)
    tile_list = draw_tile_list(jax.random.fold_in(seeds[4], 71), 0)
    return {"pivot_inverse": pivot_inverse, "panel": panel, "trailing": trailing, "tile_list": tile_list}


highest = lax.Precision.HIGHEST


def reference(pivot_inverse, panel, trailing, tile_list):
    solved = jnp.einsum("pak,jk->paj", panel, pivot_inverse, precision=highest)
    group_index = jnp.arange(TRAIL, dtype=jnp.int32) // TR_DEV
    row_tile = (group_index * PAN_DEV + tile_list[:, 0]).astype(jnp.int32)
    col_tile = jnp.maximum(tile_list[:, 1], 0).astype(jnp.int32)
    live_slot = tile_list[:, 1] >= 0

    def update_slot(packed):
        current, left_index, right_index, live_flag = packed
        product = jnp.einsum("ak,bk->ab", solved[left_index], solved[right_index], precision=highest)
        return current - jnp.where(live_flag, product, jnp.zeros_like(product))

    updated = lax.map(update_slot, (trailing, row_tile, col_tile, live_slot))
    return solved, updated
```

```python
import functools

import jax
import jax.numpy as jnp
from jax import lax
from jax.experimental import pallas as pl
from jax.experimental.pallas import tpu as pltpu
from jax.sharding import PartitionSpec as P

MESH = pl.DeviceIdType.MESH
LIGHT = 6
CHUNKS = 4
f32, bf16 = jnp.float32, jnp.bfloat16


def halves(x):
    hi = x.astype(bf16)
    return hi, (x - hi.astype(f32)).astype(bf16)


def dot_nt(a, b):
    return lax.dot_general(a, b, (((1,), (1,)), ((), ())), preferred_element_type=f32)


def dot_nn(a, b):
    return lax.dot_general(a, b, (((1,), (0,)), ((), ())), preferred_element_type=f32)


def table(index, values):
    found = jnp.int32(0)
    for at, value in enumerate(values):
        found = jnp.where(index == at, jnp.int32(value), found)
    return found


def kernel(rows, cols, pivot, panel, trailing, tiles, solved, updated,
           sl, q, factor, own_hi, own_lo, solved_buf, q3, acc,
           load_sem, in_sem, out_sem, solved_sem,
           lz_recv, lz_send, lr_recv, lr_send, ls_recv, ls_send,
           row_recv, row_send, sib_recv, sib_send, q_recv, q_send):
    chips = rows // 2
    pan, height, order = panel.shape
    slots = trailing.shape[0]
    kc = order // CHUNKS
    far = cols // 2
    rest = 3 if chips > 3 else chips
    ring = [i ^ (i >> 1) for i in range(cols)]
    where_in = [ring.index(i) for i in range(cols)]

    row, col = lax.axis_index("row"), lax.axis_index("col")
    chip, core = lax.div(row, 2), lax.rem(row, 2)
    spot = table(col, where_in)

    def ring_col(step):
        return table(lax.rem(spot + step + cols, cols), ring)

    above, below = (row + 2, col), (row - 2, col)
    sibling = (chip * 2 + 1 - core, col)
    ahead, behind = (row, ring_col(1)), (row, ring_col(-1))
    has_above, has_below = chip < chips - 1, chip > 0
    live = jnp.where(row < rows // 2, jnp.int32(min(LIGHT, slots)), jnp.int32(slots))

    def own_panel(c):
        return pltpu.make_async_copy(
            panel.at[:, :, pl.ds(c * kc, kc)], sl[c].at[pl.ds(row * pan, pan)], load_sem.at[c])

    share = pivot.shape[0] // cols
    own_factor = pltpu.make_async_copy(
        pivot.at[pl.ds(pl.multiple_of(col * share, share), share)], factor.at[core, col, chip], load_sem.at[CHUNKS])
    own_factor.start()
    for c in range(CHUNKS):
        own_panel(c).start()

    def slot_in(t):
        return pltpu.make_async_copy(trailing.at[t], acc.at[t], in_sem.at[t])

    def slot_out(t):
        return pltpu.make_async_copy(acc.at[t], updated.at[t], out_sem.at[t])

    def slot_pass(t):
        return pltpu.make_async_copy(trailing.at[t], updated.at[t], out_sem.at[t])

    def over(lo, hi, act):
        def body(t, carry):
            act(t)
            return carry
        lax.fori_loop(lo, hi, body, 0)

    barrier = pltpu.get_barrier_semaphore()
    for other in (sibling, ahead, behind):
        pl.semaphore_signal(barrier, inc=1, device_id=other, device_id_type=MESH)

    @pl.when(has_above)
    def _():
        pl.semaphore_signal(barrier, inc=1, device_id=above, device_id_type=MESH)

    @pl.when(has_below)
    def _():
        pl.semaphore_signal(barrier, inc=1, device_id=below, device_id_type=MESH)

    pl.semaphore_wait(barrier, 3 + jnp.where(has_above, 1, 0) + jnp.where(has_below, 1, 0))

    def remote(ref, send, recv, device):
        return pltpu.make_async_remote_copy(
            src_ref=ref, dst_ref=ref, send_sem=send, recv_sem=recv, device_id=device, device_id_type=MESH)

    def factor_line(up, src):
        return remote(factor.at[core, col, src], lz_send.at[0 if up else 1, src], lz_recv.at[src], above if up else below)

    hc = chips // 2

    def factor_part(side, at, h):
        return factor.at[side, at, pl.ds(h * hc, hc)]

    def factor_ring(fwd, at, h):
        return remote(factor_part(core, at, h), lr_send.at[0 if fwd else 1, at, h], lr_recv.at[at, h], ahead if fwd else behind)

    def factor_sib(side, at, h):
        return remote(factor_part(side, at, h), ls_send.at[at, h], ls_recv.at[at, h], sibling)

    def slices_of(c, src, side):
        return sl[c].at[pl.ds((src * 2 + side) * pan, pan)]

    def row_line(c, up, src):
        return remote(slices_of(c, src, core), row_send.at[c, 0 if up else 1, src], row_recv.at[c, src], above if up else below)

    def row_sib(c, src, side):
        return remote(slices_of(c, src, side), sib_send.at[c, src], sib_recv.at[c, src], sibling)

    def q_ring(c, fwd, at, h):
        return remote(q[c].at[h, at], q_send.at[c, 0 if fwd else 1, at, h], q_recv.at[c, at, h], ahead if fwd else behind)

    def line_own(make):
        @pl.when(has_above)
        def _():
            make(True, chip).start()

        @pl.when(has_below)
        def _():
            make(False, chip).start()

    def line_event(make, d, also):
        @pl.when(chip - d >= 0)
        def _():
            make(True, chip - d).wait_recv()

            @pl.when(has_above)
            def _():
                make(True, chip - d).start()
            also(chip - d)

        @pl.when(chip + d < chips)
        def _():
            make(False, chip + d).wait_recv()

            @pl.when(has_below)
            def _():
                make(False, chip + d).start()
            also(chip + d)

    def line_drain(make):
        @pl.when(has_above)
        def _():
            over(0, chip + 1, lambda src: make(True, src).wait_send())

        @pl.when(has_below)
        def _():
            over(chip, chips, lambda src: make(False, src).wait_send())

    def goes(d, fwd, h, count):
        return d < far or (d == far and (2 * h < count) == fwd)

    def ring_event(make, d, count, also):
        for h in range(count):
            for fwd in (True, False):
                if goes(d, fwd, h, count):
                    at = ring_col(-d if fwd else d)
                    if d > 0:
                        make(fwd, at, h).wait_recv()
                    if goes(d + 1, fwd, h, count):
                        make(fwd, at, h).start()
                    if d > 0:
                        also(at, h)

    def ring_drain(make, count):
        for d in range(far):
            for h in range(count):
                for fwd in (True, False):
                    if goes(d + 1, fwd, h, count):
                        make(fwd, ring_col(-d if fwd else d), h).wait_send()

    def row_own(c):
        line_own(functools.partial(row_line, c))
        row_sib(c, chip, core).start()

    def row_event(c, lo, hi):
        for d in range(lo, hi):
            line_event(functools.partial(row_line, c), d, lambda src: row_sib(c, src, core).start())

    def q_event(c, d):
        ring_event(functools.partial(q_ring, c), d, pan, lambda at, h: None)

    own_factor.wait()
    line_own(factor_line)
    own_panel(0).wait()
    row_own(0)
    over(0, live, lambda t: slot_in(t).start())
    over(live, slots, lambda t: slot_pass(t).start())
    for c in range(1, CHUNKS):
        own_panel(c).wait()

    for c in range(CHUNKS):
        hi, lo = halves(sl[c][pl.ds(row * pan, pan)].reshape(pan * height, kc))
        own_hi[:, c * kc:(c + 1) * kc] = hi
        own_lo[:, c * kc:(c + 1) * kc] = lo

    for d in range(1, chips):
        line_event(factor_line, d, lambda src: None)
    row_own(1)

    def pass_factor(at, h):
        factor_sib(core, at, h).start()

    ring_event(factor_ring, 0, 2, pass_factor)
    for h in range(2):
        pass_factor(col, h)
    row_event(0, 1, 2)
    ring_event(factor_ring, 1, 2, pass_factor)
    row_event(0, 2, rest)
    for d in range(2, far + 1):
        ring_event(factor_ring, d, 2, pass_factor)
    row_own(2)
    for at in range(cols):
        for h in range(2):
            factor_sib(1 - core, at, h).wait_recv()
    row_event(1, 1, 2)

    block = order // chips
    for b in range(chips):
        depth = min(order, -(-((b + 1) * block) // 128) * 128)
        l_hi, l_lo = halves(factor[:, :, b, :, :depth].reshape(block, depth))
        a_hi, a_lo = own_hi[:, :depth], own_lo[:, :depth]
        part = dot_nt(a_hi, l_hi) + (dot_nt(a_hi, l_lo) + dot_nt(a_lo, l_hi))
        solved_buf[:, :, b * block:(b + 1) * block] = part.reshape(pan, height, block)
    solved_copy = pltpu.make_async_copy(solved_buf, solved, solved_sem)
    for b in range(CHUNKS):
        hi, lo = halves(solved_buf[:, :, b * kc:(b + 1) * kc].reshape(pan * height, kc))
        own_hi[:, b * kc:(b + 1) * kc] = hi
        own_lo[:, b * kc:(b + 1) * kc] = lo
    solved_copy.start()

    for c in range(CHUNKS):
        first = (c * kc) // block
        span = pl.ds(c * kc, kc)
        l_rows = jnp.concatenate([factor[:, :, b, :, span].reshape(block, kc) for b in range(first, chips)], axis=0)
        l_hi, l_lo = halves(l_rows)
        s_hi, s_lo = own_hi[:, first * block:], own_lo[:, first * block:]
        part = dot_nn(s_hi, l_hi) + (dot_nn(s_hi, l_lo) + dot_nn(s_lo, l_hi))
        part = part.reshape(pan, height, kc)
        for h in range(pan):
            q[c][h, col] = part[h]
        q_event(c, 0)
        if c == 1:
            row_event(1, 2, rest)
    row_own(3)
    q_event(0, 1)

    def update(c, part, parts):
        def one(t):
            left = q3[tiles[t, 0]]
            r_hi, r_lo = halves(sl[c][tiles[t, 1]])
            right = jnp.concatenate([r_hi, r_lo, r_hi], axis=1)
            if c == 0:
                slot_in(t).wait()
            acc[t] = acc[t] - dot_nt(left, right)
            if c == CHUNKS - 1:
                slot_out(t).start()
        over(live * part // parts, live * (part + 1) // parts, one)

    for c in range(CHUNKS):
        for d in range(2, far + 1):
            q_event(c, d)
        if c + 1 < CHUNKS:
            q_event(c + 1, 1)
        for h in range(pan):
            hi, lo = halves(q[c][h].reshape(cols * height, kc))
            q3[h, :, 0:kc] = hi
            q3[h, :, kc:2 * kc] = hi
            q3[h, :, 2 * kc:3 * kc] = lo
        row_event(c, rest, chips)
        over(0, chips, lambda src: row_sib(c, src, 1 - core).wait_recv())
        update(c, 0, 2)
        if c + 2 < CHUNKS:
            row_event(c + 2, 1, 2)
        update(c, 1, 2)
        if c + 2 < CHUNKS:
            row_event(c + 2, 2, rest)

    line_drain(factor_line)
    ring_drain(factor_ring, 2)
    for at in range(cols):
        for h in range(2):
            factor_sib(core, at, h).wait_send()
    for c in range(CHUNKS):
        line_drain(functools.partial(row_line, c))
        over(0, chips, lambda src: row_sib(c, src, core).wait_send())
        ring_drain(functools.partial(q_ring, c), pan)
    solved_copy.wait()
    over(0, live, lambda t: slot_out(t).wait())
    over(live, slots, lambda t: slot_pass(t).wait())


def per_device(rows, cols, pivot_inverse, panel, trailing, tile_list):
    pan, height, order = panel.shape
    slots, _, width = trailing.shape
    chips, kc = rows // 2, order // CHUNKS
    share = pivot_inverse.shape[0] // cols
    dma = pltpu.SemaphoreType.DMA
    anywhere = pl.BlockSpec(memory_space=pltpu.HBM)
    return pl.pallas_call(
        functools.partial(kernel, rows, cols),
        out_shape=(
            jax.ShapeDtypeStruct(panel.shape, f32),
            jax.ShapeDtypeStruct(trailing.shape, f32),
        ),
        in_specs=[anywhere, anywhere, anywhere, pl.BlockSpec(memory_space=pltpu.SMEM)],
        out_specs=(anywhere, anywhere),
        scratch_shapes=[
            [pltpu.VMEM((rows * pan, height, kc), f32) for _ in range(CHUNKS)],
            [pltpu.VMEM((pan, cols, height, kc), f32) for _ in range(CHUNKS)],
            pltpu.VMEM((2, cols, chips, share, order), f32),
            pltpu.VMEM((pan * height, order), bf16),
            pltpu.VMEM((pan * height, order), bf16),
            pltpu.VMEM((pan, height, order), f32),
            pltpu.VMEM((pan, cols * height, 3 * kc), bf16),
            pltpu.VMEM((slots, order, width), f32),
            dma((CHUNKS + 1,)),
            dma((slots,)),
            dma((slots,)),
            dma(()),
            dma((chips,)),
            dma((2, chips)),
            dma((cols, 2)),
            dma((2, cols, 2)),
            dma((cols, 2)),
            dma((cols, 2)),
            dma((CHUNKS, chips)),
            dma((CHUNKS, 2, chips)),
            dma((CHUNKS, chips)),
            dma((CHUNKS, chips)),
            dma((CHUNKS, cols, pan)),
            dma((CHUNKS, 2, cols, pan)),
        ],
        compiler_params=pltpu.CompilerParams(
            collective_id=0, has_side_effects=True, vmem_limit_bytes=67043328
        ),
    )(pivot_inverse, panel, trailing, tile_list)


def solution(mesh):
    placed = (P("row", None), P("row", "col", None), P("row", None, "col"), P("row", None))
    return jax.shard_map(
        functools.partial(per_device, mesh.shape["row"], mesh.shape["col"]),
        mesh=mesh,
        in_specs=placed,
        out_specs=(P("row", "col", None), P("row", None, "col")),
        check_vma=False,
    )
```

```python
import functools

import jax
import jax.numpy as jnp
from jax import lax
from jax.experimental import pallas as pl
from jax.experimental.pallas import tpu as pltpu
from jax.sharding import PartitionSpec as P

MESH = pl.DeviceIdType.MESH
LIGHT = 6
CHUNKS = 4
f32, bf16 = jnp.float32, jnp.bfloat16


def halves(x):
    hi = x.astype(bf16)
    return hi, (x - hi.astype(f32)).astype(bf16)


def dot_nt(a, b):
    return lax.dot_general(a, b, (((1,), (1,)), ((), ())), preferred_element_type=f32)


def dot_nn(a, b):
    return lax.dot_general(a, b, (((1,), (0,)), ((), ())), preferred_element_type=f32)


def table(index, values):
    found = jnp.int32(0)
    for at, value in enumerate(values):
        found = jnp.where(index == at, jnp.int32(value), found)
    return found


def kernel(rows, cols, pivot, panel, trailing, tiles, solved, updated,
           sl, q, factor, own_hi, own_lo, solved_buf, q3, acc,
           load_sem, in_sem, out_sem, solved_sem,
           lz_recv, lz_send, lr_recv, lr_send, ls_recv, ls_send,
           row_recv, row_send, sib_recv, sib_send, q_recv, q_send):
    chips = rows // 2
    pan, height, order = panel.shape
    slots = trailing.shape[0]
    kc = order // CHUNKS
    far = cols // 2
    rest = 3 if chips > 3 else chips
    ring = [i ^ (i >> 1) for i in range(cols)]
    where_in = [ring.index(i) for i in range(cols)]

    row, col = lax.axis_index("row"), lax.axis_index("col")
    chip, core = lax.div(row, 2), lax.rem(row, 2)
    spot = table(col, where_in)

    def ring_col(step):
        return table(lax.rem(spot + step + cols, cols), ring)

    above, below = (row + 2, col), (row - 2, col)
    sibling = (chip * 2 + 1 - core, col)
    ahead, behind = (row, ring_col(1)), (row, ring_col(-1))
    has_above, has_below = chip < chips - 1, chip > 0
    live = jnp.where(row < rows // 2, jnp.int32(min(LIGHT, slots)), jnp.int32(slots))

    def own_panel(c):
        return pltpu.make_async_copy(
            panel.at[:, :, pl.ds(c * kc, kc)], sl[c].at[pl.ds(row * pan, pan)], load_sem.at[c])

    share = pivot.shape[0] // cols
    own_factor = pltpu.make_async_copy(
        pivot.at[pl.ds(pl.multiple_of(col * share, share), share)], factor.at[core, col, chip], load_sem.at[CHUNKS])
    own_factor.start()
    for c in range(CHUNKS):
        own_panel(c).start()

    def slot_in(t):
        return pltpu.make_async_copy(trailing.at[t], acc.at[t], in_sem.at[t])

    def slot_out(t):
        return pltpu.make_async_copy(acc.at[t], updated.at[t], out_sem.at[t])

    def over(lo, hi, act):
        def body(t, carry):
            act(t)
            return carry
        lax.fori_loop(lo, hi, body, 0)

    barrier = pltpu.get_barrier_semaphore()
    for other in (sibling, ahead, behind):
        pl.semaphore_signal(barrier, inc=1, device_id=other, device_id_type=MESH)

    @pl.when(has_above)
    def _():
        pl.semaphore_signal(barrier, inc=1, device_id=above, device_id_type=MESH)

    @pl.when(has_below)
    def _():
        pl.semaphore_signal(barrier, inc=1, device_id=below, device_id_type=MESH)

    pl.semaphore_wait(barrier, 3 + jnp.where(has_above, 1, 0) + jnp.where(has_below, 1, 0))

    def remote(ref, send, recv, device):
        return pltpu.make_async_remote_copy(
            src_ref=ref, dst_ref=ref, send_sem=send, recv_sem=recv, device_id=device, device_id_type=MESH)

    def factor_line(up, src):
        return remote(factor.at[core, col, src], lz_send.at[0 if up else 1, src], lz_recv.at[src], above if up else below)

    hc = chips // 2

    def factor_part(side, at, h):
        return factor.at[side, at, pl.ds(h * hc, hc)]

    def factor_ring(fwd, at, h):
        return remote(factor_part(core, at, h), lr_send.at[0 if fwd else 1, at, h], lr_recv.at[at, h], ahead if fwd else behind)

    def factor_sib(side, at, h):
        return remote(factor_part(side, at, h), ls_send.at[at, h], ls_recv.at[at, h], sibling)

    def slices_of(c, src, side):
        return sl[c].at[pl.ds((src * 2 + side) * pan, pan)]

    def row_line(c, up, src):
        return remote(slices_of(c, src, core), row_send.at[c, 0 if up else 1, src], row_recv.at[c, src], above if up else below)

    def row_sib(c, src, side):
        return remote(slices_of(c, src, side), sib_send.at[c, src], sib_recv.at[c, src], sibling)

    def q_ring(c, fwd, at, h):
        return remote(q[c].at[h, at], q_send.at[c, 0 if fwd else 1, at, h], q_recv.at[c, at, h], ahead if fwd else behind)

    def line_own(make):
        @pl.when(has_above)
        def _():
            make(True, chip).start()

        @pl.when(has_below)
        def _():
            make(False, chip).start()

    def line_event(make, d, also):
        @pl.when(chip - d >= 0)
        def _():
            make(True, chip - d).wait_recv()

            @pl.when(has_above)
            def _():
                make(True, chip - d).start()
            also(chip - d)

        @pl.when(chip + d < chips)
        def _():
            make(False, chip + d).wait_recv()

            @pl.when(has_below)
            def _():
                make(False, chip + d).start()
            also(chip + d)

    def line_drain(make):
        @pl.when(has_above)
        def _():
            over(0, chip + 1, lambda src: make(True, src).wait_send())

        @pl.when(has_below)
        def _():
            over(chip, chips, lambda src: make(False, src).wait_send())

    def goes(d, fwd, h, count):
        return d < far or (d == far and (2 * h < count) == fwd)

    def ring_event(make, d, count, also):
        for h in range(count):
            for fwd in (True, False):
                if goes(d, fwd, h, count):
                    at = ring_col(-d if fwd else d)
                    if d > 0:
                        make(fwd, at, h).wait_recv()
                    if goes(d + 1, fwd, h, count):
                        make(fwd, at, h).start()
                    if d > 0:
                        also(at, h)

    def ring_drain(make, count):
        for d in range(far):
            for h in range(count):
                for fwd in (True, False):
                    if goes(d + 1, fwd, h, count):
                        make(fwd, ring_col(-d if fwd else d), h).wait_send()

    def row_own(c):
        line_own(functools.partial(row_line, c))
        row_sib(c, chip, core).start()

    def row_event(c, lo, hi):
        for d in range(lo, hi):
            line_event(functools.partial(row_line, c), d, lambda src: row_sib(c, src, core).start())

    def q_event(c, d):
        ring_event(functools.partial(q_ring, c), d, pan, lambda at, h: None)

    own_factor.wait()
    line_own(factor_line)
    own_panel(0).wait()
    row_own(0)
    over(0, slots, lambda t: slot_in(t).start())
    for c in range(1, CHUNKS):
        own_panel(c).wait()

    for c in range(CHUNKS):
        hi, lo = halves(sl[c][pl.ds(row * pan, pan)].reshape(pan * height, kc))
        own_hi[:, c * kc:(c + 1) * kc] = hi
        own_lo[:, c * kc:(c + 1) * kc] = lo

    for d in range(1, chips):
        line_event(factor_line, d, lambda src: None)
    row_own(1)

    def untouched(t):
        slot_in(t).wait()
        slot_out(t).start()

    over(live, slots, untouched)

    def pass_factor(at, h):
        factor_sib(core, at, h).start()

    ring_event(factor_ring, 0, 2, pass_factor)
    for h in range(2):
        pass_factor(col, h)
    row_event(0, 1, 2)
    ring_event(factor_ring, 1, 2, pass_factor)
    row_event(0, 2, rest)
    for d in range(2, far + 1):
        ring_event(factor_ring, d, 2, pass_factor)
    row_own(2)
    for at in range(cols):
        for h in range(2):
            factor_sib(1 - core, at, h).wait_recv()
    row_event(1, 1, 2)

    block = order // chips
    for b in range(chips):
        depth = min(order, -(-((b + 1) * block) // 128) * 128)
        l_hi, l_lo = halves(factor[:, :, b, :, :depth].reshape(block, depth))
        a_hi, a_lo = own_hi[:, :depth], own_lo[:, :depth]
        part = dot_nt(a_hi, l_hi) + (dot_nt(a_hi, l_lo) + dot_nt(a_lo, l_hi))
        solved_buf[:, :, b * block:(b + 1) * block] = part.reshape(pan, height, block)
    solved_copy = pltpu.make_async_copy(solved_buf, solved, solved_sem)
    for b in range(CHUNKS):
        hi, lo = halves(solved_buf[:, :, b * kc:(b + 1) * kc].reshape(pan * height, kc))
        own_hi[:, b * kc:(b + 1) * kc] = hi
        own_lo[:, b * kc:(b + 1) * kc] = lo
    solved_copy.start()

    for c in range(CHUNKS):
        first = (c * kc) // block
        span = pl.ds(c * kc, kc)
        l_rows = jnp.concatenate([factor[:, :, b, :, span].reshape(block, kc) for b in range(first, chips)], axis=0)
        l_hi, l_lo = halves(l_rows)
        s_hi, s_lo = own_hi[:, first * block:], own_lo[:, first * block:]
        part = dot_nn(s_hi, l_hi) + (dot_nn(s_hi, l_lo) + dot_nn(s_lo, l_hi))
        part = part.reshape(pan, height, kc)
        for h in range(pan):
            q[c][h, col] = part[h]
        q_event(c, 0)
        if c == 1:
            row_event(1, 2, rest)
    row_own(3)
    q_event(0, 1)

    def update(c, part, parts):
        def one(t):
            left = q3[tiles[t, 0]]
            r_hi, r_lo = halves(sl[c][tiles[t, 1]])
            right = jnp.concatenate([r_hi, r_lo, r_hi], axis=1)
            if c == 0:
                slot_in(t).wait()
            acc[t] = acc[t] - dot_nt(left, right)
            if c == CHUNKS - 1:
                slot_out(t).start()
        over(live * part // parts, live * (part + 1) // parts, one)

    for c in range(CHUNKS):
        for d in range(2, far + 1):
            q_event(c, d)
        if c + 1 < CHUNKS:
            q_event(c + 1, 1)
        for h in range(pan):
            hi, lo = halves(q[c][h].reshape(cols * height, kc))
            q3[h, :, 0:kc] = hi
            q3[h, :, kc:2 * kc] = hi
            q3[h, :, 2 * kc:3 * kc] = lo
        row_event(c, rest, chips)
        over(0, chips, lambda src: row_sib(c, src, 1 - core).wait_recv())
        update(c, 0, 2)
        if c + 2 < CHUNKS:
            row_event(c + 2, 1, 2)
        update(c, 1, 2)
        if c + 2 < CHUNKS:
            row_event(c + 2, 2, rest)

    line_drain(factor_line)
    ring_drain(factor_ring, 2)
    for at in range(cols):
        for h in range(2):
            factor_sib(core, at, h).wait_send()
    for c in range(CHUNKS):
        line_drain(functools.partial(row_line, c))
        over(0, chips, lambda src: row_sib(c, src, core).wait_send())
        ring_drain(functools.partial(q_ring, c), pan)
    solved_copy.wait()
    over(0, slots, lambda t: slot_out(t).wait())


def per_device(rows, cols, pivot_inverse, panel, trailing, tile_list):
    pan, height, order = panel.shape
    slots, _, width = trailing.shape
    chips, kc = rows // 2, order // CHUNKS
    share = pivot_inverse.shape[0] // cols
    dma = pltpu.SemaphoreType.DMA
    anywhere = pl.BlockSpec(memory_space=pl.ANY)
    return pl.pallas_call(
        functools.partial(kernel, rows, cols),
        out_shape=(
            jax.ShapeDtypeStruct(panel.shape, f32),
            jax.ShapeDtypeStruct(trailing.shape, f32),
        ),
        in_specs=[anywhere, anywhere, anywhere, pl.BlockSpec(memory_space=pltpu.SMEM)],
        out_specs=(anywhere, anywhere),
        scratch_shapes=[
            [pltpu.VMEM((rows * pan, height, kc), f32) for _ in range(CHUNKS)],
            [pltpu.VMEM((pan, cols, height, kc), f32) for _ in range(CHUNKS)],
            pltpu.VMEM((2, cols, chips, share, order), f32),
            pltpu.VMEM((pan * height, order), bf16),
            pltpu.VMEM((pan * height, order), bf16),
            pltpu.VMEM((pan, height, order), f32),
            pltpu.VMEM((pan, cols * height, 3 * kc), bf16),
            pltpu.VMEM((slots, order, width), f32),
            dma((CHUNKS + 1,)),
            dma((slots,)),
            dma((slots,)),
            dma(()),
            dma((chips,)),
            dma((2, chips)),
            dma((cols, 2)),
            dma((2, cols, 2)),
            dma((cols, 2)),
            dma((cols, 2)),
            dma((CHUNKS, chips)),
            dma((CHUNKS, 2, chips)),
            dma((CHUNKS, chips)),
            dma((CHUNKS, chips)),
            dma((CHUNKS, cols, pan)),
            dma((CHUNKS, 2, cols, pan)),
        ],
        compiler_params=pltpu.CompilerParams(
            collective_id=0, has_side_effects=True, vmem_limit_bytes=67043328
        ),
    )(pivot_inverse, panel, trailing, tile_list)


def solution(mesh):
    placed = (P("row", None), P("row", "col", None), P("row", None, "col"), P("row", None))
    return jax.shard_map(
        functools.partial(per_device, mesh.shape["row"], mesh.shape["col"]),
        mesh=mesh,
        in_specs=placed,
        out_specs=(P("row", "col", None), P("row", None, "col")),
        check_vma=False,
    )
```

```python
import functools

import jax
import jax.numpy as jnp
from jax import lax
from jax.experimental import pallas as pl
from jax.experimental.pallas import tpu as pltpu
from jax.sharding import PartitionSpec as P

MESH = pl.DeviceIdType.MESH
LIGHT = 6
CHUNKS = 4
f32, bf16 = jnp.float32, jnp.bfloat16


def halves(x):
    hi = x.astype(bf16)
    return hi, (x - hi.astype(f32)).astype(bf16)


def dot_nt(a, b):
    return lax.dot_general(a, b, (((1,), (1,)), ((), ())), preferred_element_type=f32)


def dot_nn(a, b):
    return lax.dot_general(a, b, (((1,), (0,)), ((), ())), preferred_element_type=f32)


def table(index, values):
    found = jnp.int32(0)
    for at, value in enumerate(values):
        found = jnp.where(index == at, jnp.int32(value), found)
    return found


def kernel(rows, cols, pivot, panel, trailing, tiles, solved, updated, last_slices, last_left,
           sl, q, factor, own_hi, own_lo, solved_buf, q3, acc,
           load_sem, in_sem, out_sem, solved_sem, last_sem,
           lz_recv, lz_send, lr_recv, lr_send, ls_recv, ls_send,
           row_recv, row_send, sib_recv, sib_send, q_recv, q_send):
    chips = rows // 2
    pan, height, order = panel.shape
    slots = trailing.shape[0]
    kc = order // CHUNKS
    far = cols // 2
    rest = 3 if chips > 3 else chips
    ring = [i ^ (i >> 1) for i in range(cols)]
    where_in = [ring.index(i) for i in range(cols)]

    row, col = lax.axis_index("row"), lax.axis_index("col")
    chip, core = lax.div(row, 2), lax.rem(row, 2)
    spot = table(col, where_in)

    def ring_col(step):
        return table(lax.rem(spot + step + cols, cols), ring)

    above, below = (row + 2, col), (row - 2, col)
    sibling = (chip * 2 + 1 - core, col)
    ahead, behind = (row, ring_col(1)), (row, ring_col(-1))
    has_above, has_below = chip < chips - 1, chip > 0
    live = jnp.where(row < rows // 2, jnp.int32(min(LIGHT, slots)), jnp.int32(slots))

    def own_panel(c):
        return pltpu.make_async_copy(
            panel.at[:, :, pl.ds(c * kc, kc)], sl[c].at[pl.ds(row * pan, pan)], load_sem.at[c])

    share = pivot.shape[0] // cols
    own_factor = pltpu.make_async_copy(
        pivot.at[pl.ds(pl.multiple_of(col * share, share), share)], factor.at[core, col, chip], load_sem.at[CHUNKS])
    own_factor.start()
    for c in range(CHUNKS):
        own_panel(c).start()

    def slot_in(t):
        return pltpu.make_async_copy(trailing.at[t], acc.at[t], in_sem.at[t])

    def slot_out(t):
        return pltpu.make_async_copy(acc.at[t], updated.at[t], out_sem.at[t])

    def over(lo, hi, act):
        def body(t, carry):
            act(t)
            return carry
        lax.fori_loop(lo, hi, body, 0)

    barrier = pltpu.get_barrier_semaphore()
    for other in (sibling, ahead, behind):
        pl.semaphore_signal(barrier, inc=1, device_id=other, device_id_type=MESH)

    @pl.when(has_above)
    def _():
        pl.semaphore_signal(barrier, inc=1, device_id=above, device_id_type=MESH)

    @pl.when(has_below)
    def _():
        pl.semaphore_signal(barrier, inc=1, device_id=below, device_id_type=MESH)

    pl.semaphore_wait(barrier, 3 + jnp.where(has_above, 1, 0) + jnp.where(has_below, 1, 0))

    def remote(ref, send, recv, device):
        return pltpu.make_async_remote_copy(
            src_ref=ref, dst_ref=ref, send_sem=send, recv_sem=recv, device_id=device, device_id_type=MESH)

    def factor_line(up, src):
        return remote(factor.at[core, col, src], lz_send.at[0 if up else 1, src], lz_recv.at[src], above if up else below)

    hc = chips // 2

    def factor_part(side, at, h):
        return factor.at[side, at, pl.ds(h * hc, hc)]

    def factor_ring(fwd, at, h):
        return remote(factor_part(core, at, h), lr_send.at[0 if fwd else 1, at, h], lr_recv.at[at, h], ahead if fwd else behind)

    def factor_sib(side, at, h):
        return remote(factor_part(side, at, h), ls_send.at[at, h], ls_recv.at[at, h], sibling)

    def slices_of(c, src, side):
        return sl[c].at[pl.ds((src * 2 + side) * pan, pan)]

    def row_line(c, up, src):
        return remote(slices_of(c, src, core), row_send.at[c, 0 if up else 1, src], row_recv.at[c, src], above if up else below)

    def row_sib(c, src, side):
        return remote(slices_of(c, src, side), sib_send.at[c, src], sib_recv.at[c, src], sibling)

    def q_ring(c, fwd, at, h):
        return remote(q[c].at[h, at], q_send.at[c, 0 if fwd else 1, at, h], q_recv.at[c, at, h], ahead if fwd else behind)

    def line_own(make):
        @pl.when(has_above)
        def _():
            make(True, chip).start()

        @pl.when(has_below)
        def _():
            make(False, chip).start()

    def line_event(make, d, also):
        @pl.when(chip - d >= 0)
        def _():
            make(True, chip - d).wait_recv()

            @pl.when(has_above)
            def _():
                make(True, chip - d).start()
            also(chip - d)

        @pl.when(chip + d < chips)
        def _():
            make(False, chip + d).wait_recv()

            @pl.when(has_below)
            def _():
                make(False, chip + d).start()
            also(chip + d)

    def line_drain(make):
        @pl.when(has_above)
        def _():
            over(0, chip + 1, lambda src: make(True, src).wait_send())

        @pl.when(has_below)
        def _():
            over(chip, chips, lambda src: make(False, src).wait_send())

    def goes(d, fwd, h, count):
        return d < far or (d == far and (2 * h < count) == fwd)

    def ring_event(make, d, count, also):
        for h in range(count):
            for fwd in (True, False):
                if goes(d, fwd, h, count):
                    at = ring_col(-d if fwd else d)
                    if d > 0:
                        make(fwd, at, h).wait_recv()
                    if goes(d + 1, fwd, h, count):
                        make(fwd, at, h).start()
                    if d > 0:
                        also(at, h)

    def ring_drain(make, count):
        for d in range(far):
            for h in range(count):
                for fwd in (True, False):
                    if goes(d + 1, fwd, h, count):
                        make(fwd, ring_col(-d if fwd else d), h).wait_send()

    def row_own(c):
        line_own(functools.partial(row_line, c))
        row_sib(c, chip, core).start()

    def row_event(c, lo, hi):
        for d in range(lo, hi):
            line_event(functools.partial(row_line, c), d, lambda src: row_sib(c, src, core).start())

    def q_event(c, d):
        ring_event(functools.partial(q_ring, c), d, pan, lambda at, h: None)

    own_factor.wait()
    line_own(factor_line)
    own_panel(0).wait()
    row_own(0)
    over(0, slots, lambda t: slot_in(t).start())
    for c in range(1, CHUNKS):
        own_panel(c).wait()

    for c in range(CHUNKS):
        hi, lo = halves(sl[c][pl.ds(row * pan, pan)].reshape(pan * height, kc))
        own_hi[:, c * kc:(c + 1) * kc] = hi
        own_lo[:, c * kc:(c + 1) * kc] = lo

    for d in range(1, chips):
        line_event(factor_line, d, lambda src: None)
    row_own(1)

    def untouched(t):
        slot_in(t).wait()
        slot_out(t).start()

    over(live, slots, untouched)

    def pass_factor(at, h):
        factor_sib(core, at, h).start()

    ring_event(factor_ring, 0, 2, pass_factor)
    for h in range(2):
        pass_factor(col, h)
    row_event(0, 1, 2)
    ring_event(factor_ring, 1, 2, pass_factor)
    row_event(0, 2, rest)
    for d in range(2, far + 1):
        ring_event(factor_ring, d, 2, pass_factor)
    row_own(2)
    for at in range(cols):
        for h in range(2):
            factor_sib(1 - core, at, h).wait_recv()
    row_event(1, 1, 2)

    block = order // chips
    for b in range(chips):
        depth = min(order, -(-((b + 1) * block) // 128) * 128)
        l_hi, l_lo = halves(factor[:, :, b, :, :depth].reshape(block, depth))
        a_hi, a_lo = own_hi[:, :depth], own_lo[:, :depth]
        part = dot_nt(a_hi, l_hi) + (dot_nt(a_hi, l_lo) + dot_nt(a_lo, l_hi))
        solved_buf[:, :, b * block:(b + 1) * block] = part.reshape(pan, height, block)
    solved_copy = pltpu.make_async_copy(solved_buf, solved, solved_sem)
    for b in range(CHUNKS):
        hi, lo = halves(solved_buf[:, :, b * kc:(b + 1) * kc].reshape(pan * height, kc))
        own_hi[:, b * kc:(b + 1) * kc] = hi
        own_lo[:, b * kc:(b + 1) * kc] = lo
    solved_copy.start()

    for c in range(CHUNKS):
        first = (c * kc) // block
        span = pl.ds(c * kc, kc)
        l_rows = jnp.concatenate([factor[:, :, b, :, span].reshape(block, kc) for b in range(first, chips)], axis=0)
        l_hi, l_lo = halves(l_rows)
        s_hi, s_lo = own_hi[:, first * block:], own_lo[:, first * block:]
        part = dot_nn(s_hi, l_hi) + (dot_nn(s_hi, l_lo) + dot_nn(s_lo, l_hi))
        part = part.reshape(pan, height, kc)
        for h in range(pan):
            q[c][h, col] = part[h]
        q_event(c, 0)
        if c == 1:
            row_event(1, 2, rest)
    row_own(3)
    q_event(0, 1)

    def update(c, part, parts):
        def one(t):
            left = q3[tiles[t, 0]]
            r_hi, r_lo = halves(sl[c][tiles[t, 1]])
            right = jnp.concatenate([r_hi, r_lo, r_hi], axis=1)
            if c == 0:
                slot_in(t).wait()
            acc[t] = acc[t] - dot_nt(left, right)
            if c == CHUNKS - 2:
                slot_out(t).start()
        over(live * part // parts, live * (part + 1) // parts, one)

    for c in range(CHUNKS):
        for d in range(2, far + 1):
            q_event(c, d)
        if c + 1 < CHUNKS:
            q_event(c + 1, 1)
        for h in range(pan):
            hi, lo = halves(q[c][h].reshape(cols * height, kc))
            q3[h, :, 0:kc] = hi
            q3[h, :, kc:2 * kc] = hi
            q3[h, :, 2 * kc:3 * kc] = lo
        row_event(c, rest, chips)
        over(0, chips, lambda src: row_sib(c, src, 1 - core).wait_recv())
        if c == CHUNKS - 1:
            break
        update(c, 0, 2)
        if c + 2 < CHUNKS:
            row_event(c + 2, 1, 2)
        update(c, 1, 2)
        if c + 2 < CHUNKS:
            row_event(c + 2, 2, rest)

    keep = (pltpu.make_async_copy(sl[CHUNKS - 1], last_slices, last_sem.at[0]),
            pltpu.make_async_copy(q3, last_left, last_sem.at[1]))
    for copy in keep:
        copy.start()

    line_drain(factor_line)
    ring_drain(factor_ring, 2)
    for at in range(cols):
        for h in range(2):
            factor_sib(core, at, h).wait_send()
    for c in range(CHUNKS):
        line_drain(functools.partial(row_line, c))
        over(0, chips, lambda src: row_sib(c, src, core).wait_send())
        ring_drain(functools.partial(q_ring, c), pan)
    solved_copy.wait()
    for copy in keep:
        copy.wait()
    over(0, slots, lambda t: slot_out(t).wait())


def closing(tiles, partial, slices, lefts, out):
    t = pl.program_id(0)

    @pl.when(tiles[t, 1] >= 0)
    def _():
        r_hi, r_lo = halves(slices[tiles[t, 1]])
        right = jnp.concatenate([r_hi, r_lo, r_hi], axis=1)
        out[0] = partial[0] - dot_nt(lefts[tiles[t, 0]], right)

    @pl.when(tiles[t, 1] < 0)
    def _():
        out[...] = partial[...]


def per_device(rows, cols, pivot_inverse, panel, trailing, tile_list):
    pan, height, order = panel.shape
    slots, _, width = trailing.shape
    chips, kc = rows // 2, order // CHUNKS
    share = pivot_inverse.shape[0] // cols
    dma = pltpu.SemaphoreType.DMA
    anywhere = pl.BlockSpec(memory_space=pl.ANY)
    solved, partial, last_slices, last_left = pl.pallas_call(
        functools.partial(kernel, rows, cols),
        out_shape=(
            jax.ShapeDtypeStruct(panel.shape, f32),
            jax.ShapeDtypeStruct(trailing.shape, f32),
            jax.ShapeDtypeStruct((rows * pan, height, kc), f32),
            jax.ShapeDtypeStruct((pan, order, 3 * kc), bf16),
        ),
        in_specs=[anywhere, anywhere, anywhere, pl.BlockSpec(memory_space=pltpu.SMEM)],
        out_specs=(anywhere,) * 4,
        scratch_shapes=[
            [pltpu.VMEM((rows * pan, height, kc), f32) for _ in range(CHUNKS)],
            [pltpu.VMEM((pan, cols, height, kc), f32) for _ in range(CHUNKS)],
            pltpu.VMEM((2, cols, chips, share, order), f32),
            pltpu.VMEM((pan * height, order), bf16),
            pltpu.VMEM((pan * height, order), bf16),
            pltpu.VMEM((pan, height, order), f32),
            pltpu.VMEM((pan, cols * height, 3 * kc), bf16),
            pltpu.VMEM((slots, order, width), f32),
            dma((CHUNKS + 1,)),
            dma((slots,)),
            dma((slots,)),
            dma(()),
            dma((2,)),
            dma((chips,)),
            dma((2, chips)),
            dma((cols, 2)),
            dma((2, cols, 2)),
            dma((cols, 2)),
            dma((cols, 2)),
            dma((CHUNKS, chips)),
            dma((CHUNKS, 2, chips)),
            dma((CHUNKS, chips)),
            dma((CHUNKS, chips)),
            dma((CHUNKS, cols, pan)),
            dma((CHUNKS, 2, cols, pan)),
        ],
        compiler_params=pltpu.CompilerParams(
            collective_id=0, has_side_effects=True, vmem_limit_bytes=67043328
        ),
    )(pivot_inverse, panel, trailing, tile_list)
    one_slot = pl.BlockSpec((1, order, width), lambda t, tiles: (t, 0, 0))
    updated = pl.pallas_call(
        closing,
        out_shape=jax.ShapeDtypeStruct(trailing.shape, f32),
        grid_spec=pltpu.PrefetchScalarGridSpec(
            num_scalar_prefetch=1,
            grid=(slots,),
            in_specs=[
                one_slot,
                pl.BlockSpec(last_slices.shape, lambda t, tiles: (0, 0, 0)),
                pl.BlockSpec(last_left.shape, lambda t, tiles: (0, 0, 0)),
            ],
            out_specs=one_slot,
        ),
    )(tile_list, partial, last_slices, last_left)
    return solved, updated


def solution(mesh):
    placed = (P("row", None), P("row", "col", None), P("row", None, "col"), P("row", None))
    return jax.shard_map(
        functools.partial(per_device, mesh.shape["row"], mesh.shape["col"]),
        mesh=mesh,
        in_specs=placed,
        out_specs=(P("row", "col", None), P("row", None, "col")),
        check_vma=False,
    )
```
